32 devices in a mesh: batch: 4 (over z), seq: 8 (over y, x, core).
Axes of the slice: x: 2, y: 2, z: 4, core: 2. Of those that a mesh axis runs over, the one named last changes fastest.
Arguments:
- queries: bfloat16 [16384, 8, 256], P(('batch', 'seq')), parts along dimension 0, may hold values from -400 to 400
- key_heads: bfloat16 [16384, 4, 256], P(('batch', 'seq')), parts along dimension 0, may hold values from -16 to 16
- projected_value_heads: bfloat16 [16384, 4, 256], P(('batch', 'seq')), parts along dimension 0, may hold values from -6 to 6
- lengths: int32 [4], P('batch'), parts along dimension 0, may hold values from 3585 to 4096
Outputs:
- attended: bfloat16 [16384, 8, 256], P(('batch', 'seq')), parts along dimension 0
The draws below stay inside these ranges and needn't reach their ends.
There are 4 independent parts, one for each index of `batch`. The reference program is written for one: setup_inputs(seed, part) draws one part's arguments, and reference() takes and returns one part's arrays. A program takes and returns all parts, laid end to end along the dimension named above; each array names one. Nothing has to cross between parts.
All inputs are finite; a program needn't handle non-finite values.
Results may differ from the reference program's by a relative error of at most 0.0033.
Values may be sent and summed in bfloat16 or wider, within the bound.
No kernel may reach another device: no remote copies, remote signals or barrier semaphores. Data moves between devices by JAX's collectives and lax.ppermute only.
A program may use at most 192 MiB of HBM per device.

```python
import math
import jax
import jax.numpy as jnp
from jax import lax

QUERY_HEADS = 8
KEY_VALUE_HEADS = 4
HEAD_SIZE = 256
WINDOW = 4096
SINKS = 4
TOK_DEV = 512
ROW_LENGTH = 4096


def joint_draw(key):
    base = jax.random.fold_in(key, 7919)
    leading_key = jax.random.fold_in(base, 0)
    third_key = jax.random.fold_in(base, 2)
    key_value_pairs = jnp.clip(jax.random.normal(leading_key, (ROW_LENGTH, KEY_VALUE_HEADS, HEAD_SIZE), jnp.float32), -6.0, 6.0)
    query_values = 2.5 * jnp.clip(jax.random.normal(third_key, (ROW_LENGTH, QUERY_HEADS, HEAD_SIZE), jnp.float32), -6.0, 6.0)
    sink_boost = jnp.where(jnp.arange(ROW_LENGTH)[:, None, None] < SINKS, 2.0, 1.0)
    key_value_pairs = key_value_pairs * sink_boost
    return (jnp.clip(query_values, -400.0, 400.0), jnp.clip(key_value_pairs, -16.0, 16.0))


def draw_queries(key, part):
    return joint_draw(key)[0].astype(jnp.bfloat16)


def draw_key_heads(key, part):
    return joint_draw(key)[1].astype(jnp.bfloat16)


def steps_of(stream_key, shape, cuts, smallest, top_value):
    def one(position, shards_of):
        steps = jax.random.uniform(jax.random.fold_in(jax.random.fold_in(stream_key, 6), position), (shards_of,), jnp.float32, smallest / len(cuts), top_value / len(cuts))
        return jnp.repeat(jnp.exp(steps), shape[position] // shards_of).reshape((-1,) + (1,) * (len(shape) - position - 1))

    factor_of = one(*cuts[0])
    for cut in cuts[1:]:
        factor_of = factor_of * one(*cut)
    return factor_of


def scatter_about(stream_key, shape, width, most, cuts=(), kind=jnp.bfloat16):
    values = width * jax.random.normal(stream_key, shape, jnp.float32)
    if cuts:
        values = values * steps_of(stream_key, shape, cuts, -0.22, 0.18)
    return jnp.clip(values, -most, most).astype(kind)


def setup_inputs(seed: int = 0, part: int = 0) -> dict:
    streams_of = jax.random.split(jax.random.key(seed), 5)
    part_splits = jax.random.split(jax.random.fold_in(streams_of[4], part), 5)
    queries = draw_queries(jax.random.fold_in(jax.random.fold_in(streams_of[4], part), 71), part)
    key_heads = draw_key_heads(jax.random.fold_in(jax.random.fold_in(streams_of[4], part), 71), part)
    projected_value_heads = scatter_about(part_splits[2], (ROW_LENGTH, KEY_VALUE_HEADS, HEAD_SIZE), 1.0, 6.0, ((0, 8),))
    lengths = jax.random.randint(part_splits[3], (1,), ROW_LENGTH - TOK_DEV + 1, ROW_LENGTH + 1).astype(jnp.int32)
    return dict(queries=queries, key_heads=key_heads, projected_value_heads=projected_value_heads, lengths=lengths)


def reference(queries, key_heads, projected_value_heads, lengths):
    length_now = lengths[0]
    head_count = queries.shape[1]
    kv_heads = key_heads.shape[1]
    head_width = queries.shape[2]
    share = head_count // kv_heads
    block_rows = math.gcd(ROW_LENGTH, 512)
    key_span = min(ROW_LENGTH, WINDOW + block_rows)
    score_scale = head_width ** -0.5
    sink_keys = key_heads[:SINKS].astype(jnp.float32)
    sink_values = projected_value_heads[:SINKS].astype(jnp.float32)
    sink_pos = jnp.arange(SINKS, dtype=jnp.int32)

    def one_block(block_index):
        first_row = (block_index * block_rows).astype(jnp.int32)
        query_pos = first_row + jnp.arange(block_rows, dtype=jnp.int32)
        key_start = jnp.maximum(first_row + block_rows - key_span, 0).astype(jnp.int32)
        near_keys = lax.dynamic_slice_in_dim(key_heads, key_start, key_span, 0).astype(jnp.float32)
        near_values = lax.dynamic_slice_in_dim(projected_value_heads, key_start, key_span, 0).astype(jnp.float32)
        key_pos = key_start + jnp.arange(key_span, dtype=jnp.int32)
        grouped = lax.dynamic_slice_in_dim(queries, first_row, block_rows, 0).astype(jnp.float32)
        grouped = grouped.reshape(block_rows, kv_heads, share, head_width)
        all_keys = jnp.concatenate([near_keys, sink_keys], 0)
        all_values = jnp.concatenate([near_values, sink_values], 0)
        distance = query_pos[:, None] - key_pos[None, :]
        near_ok = ((distance >= 0) & (distance < WINDOW) & (key_pos[None, :] >= SINKS)
                   & (key_pos[None, :] < length_now))
        sink_gap = query_pos[:, None] - sink_pos[None, :]
        sink_ok = (sink_gap >= 0) & (sink_pos[None, :] < length_now)
        visible = jnp.concatenate([near_ok, sink_ok], 1) & (query_pos[:, None] < length_now)
        scores = jnp.einsum("qhgd,khd->hgqk", grouped, all_keys) * score_scale
        masked = jnp.where(visible, scores, -1e30)
        maximum = jnp.max(masked, axis=-1, keepdims=True)
        weights = jnp.where(visible, jnp.exp(scores - maximum), 0.0)
        totals = jnp.sum(weights, axis=-1)
        rounded = lax.optimization_barrier(weights.astype(jnp.bfloat16)).astype(jnp.float32)
        summed = jnp.einsum("hgqk,khd->hgqd", rounded, all_values)
        valid = query_pos < length_now
        result = jnp.where(valid[:, None], summed / jnp.where(valid, totals, 1.0)[..., None], 0.0)
        return result.transpose(2, 0, 1, 3).reshape(block_rows, head_count, head_width).astype(jnp.bfloat16)

    blocks = lax.map(one_block, jnp.arange(ROW_LENGTH // block_rows, dtype=jnp.int32))
    return blocks.reshape(ROW_LENGTH, head_count, head_width)
```

```python
import functools
import math

import jax
import jax.numpy as jnp
from jax import lax
from jax.experimental import pallas as pl
from jax.experimental.pallas import tpu as pltpu
from jax.sharding import PartitionSpec as P

WINDOW = 4096
SINKS = 4
NEG = -1e30


def spread(value, axis, source):
    kept = jnp.where(lax.axis_index(axis) == source, value, 0).astype(value.dtype)
    return lax.psum(kept, axis)


def windowed_shards(queries, key_heads, projected_value_heads, lengths):
    tok_rows = queries.shape[0]
    head_count = queries.shape[1]
    head_width = queries.shape[2]
    kv_heads = key_heads.shape[1]
    share = head_count // kv_heads
    position = lax.axis_index("seq")
    length_now = lengths[0]
    first_row = position * tok_rows
    score_scale = head_width ** (-0.5)
    grouped = queries.reshape(tok_rows, kv_heads, share, head_width)
    query_pos = first_row + jnp.arange(tok_rows, dtype=jnp.int32)
    last_query = first_row + tok_rows - 1

    def attend(running, kv_block, key_start, sink_mode):
        key_count = kv_block.shape[1]
        key_pos = key_start + jnp.arange(key_count, dtype=jnp.int32)
        if sink_mode:
            useful = first_row < length_now
        else:
            useful = (
                (key_start <= last_query)
                & (key_start + key_count - 1 > first_row - WINDOW)
                & (key_start < length_now)
                & (first_row < length_now)
                & (key_start + key_count > SINKS)
            )

        def compute(current):
            maximum, totals, weighted = current
            scores = (
                jnp.einsum(
                    "qhgd,khd->hgqk", grouped, kv_block[0], preferred_element_type=jnp.float32
                )
                * score_scale
            )
            distance = query_pos[:, None] - key_pos[None, :]
            if sink_mode:
                visible = (distance >= 0) & (key_pos[None, :] < length_now)
            else:
                visible = (
                    (distance >= 0)
                    & (distance < WINDOW)
                    & (key_pos[None, :] >= SINKS)
                    & (key_pos[None, :] < length_now)
                )
            visible = visible & (query_pos[:, None] < length_now)
            masked = jnp.where(visible, scores, -1e30)
            newest = jnp.maximum(maximum, jnp.max(masked, axis=-1))
            weights = jnp.where(visible, jnp.exp(scores - newest[..., None]), 0.0)
            rescale = jnp.exp(maximum - newest)
            totals = totals * rescale + jnp.sum(weights, axis=-1)
            weighted = weighted * rescale[..., None] + jnp.einsum(
                "hgqk,khd->hgqd",
                weights.astype(jnp.bfloat16),
                kv_block[1],
                preferred_element_type=jnp.float32,
            )
            return (newest, totals, weighted)

        return lax.cond(useful, compute, lambda current: current, running)

    running = (
        jnp.full((kv_heads, share, tok_rows), -1e30, jnp.float32),
        jnp.zeros((kv_heads, share, tok_rows), jnp.float32),
        jnp.zeros((kv_heads, share, tok_rows, head_width), jnp.float32),
    )
    own_pair = jnp.stack([key_heads, projected_value_heads])
    sink_pair = spread(own_pair[:, :SINKS], "seq", 0)
    running = attend(running, sink_pair, jnp.int32(0), True)
    shard_piece = lax.all_gather(own_pair, "seq", axis=1, tiled=True)
    piece_rows = shard_piece.shape[1]
    block_size = math.gcd(piece_rows, tok_rows)

    def one_slice(slice_index, inner):
        sliced = lax.dynamic_slice_in_dim(shard_piece, slice_index * block_size, block_size, 1)
        return attend(inner, sliced, slice_index * block_size, False)

    running = lax.fori_loop(0, piece_rows // block_size, one_slice, running)
    maximum, totals, weighted = running
    valid = query_pos < length_now
    result = jnp.where(valid[:, None], weighted / jnp.where(valid, totals, 1.0)[..., None], 0.0)
    return (
        result.transpose(2, 0, 1, 3).reshape(tok_rows, head_count, head_width).astype(jnp.bfloat16)
    )


def dot_nt(a, b):
    return lax.dot_general(a, b, (((1,), (1,)), ((), ())), preferred_element_type=jnp.float32)


def dot_nn(a, b):
    return lax.dot_general(a, b, (((1,), (0,)), ((), ())), preferred_element_type=jnp.float32)


def row_max(parts):
    top = jnp.max(parts[0], axis=1, keepdims=True)
    for part in parts[1:]:
        top = jnp.maximum(top, jnp.max(part, axis=1, keepdims=True))
    return top


def soft(parts, values, top, factor):
    total, out = None, None
    for part, value in zip(parts, values):
        weight = jnp.exp2((part - top) * factor)
        s = jnp.sum(weight, axis=1, keepdims=True)
        o = dot_nn(weight.astype(jnp.bfloat16), value)
        total = s if total is None else total + s
        out = o if out is None else out + o
    return total, out


def remote_kernel(tile, factor, count, active, q_hbm, *refs):
    units = refs[:count]
    out_ref, q_buf, kv_buf, sems = refs[count:]
    share, rows, width = q_buf.shape

    @pl.when(active[0] > 0)
    def _():
        copies = [pltpu.make_async_copy(q_hbm, q_buf, sems.at[0])]
        for u in range(count):
            copies.append(pltpu.make_async_copy(units[u], kv_buf.at[u], sems.at[u + 1]))
        for copy in copies:
            copy.start()
        for copy in copies:
            copy.wait()
        lane = lax.broadcasted_iota(jnp.int32, (tile, 128), 1) & 3
        pieces = []
        for j in range(rows // tile):
            block = jnp.zeros((tile, 128), jnp.float32)
            for g in range(share):
                q = q_buf[g, j * tile : (j + 1) * tile, :]
                parts = [dot_nt(q, kv_buf[u, 0]) for u in range(count)]
                top = row_max(parts)
                total, out = soft(parts, [kv_buf[u, 1] for u in range(count)], top, factor)
                at = g * rows + j * tile
                out_ref[at : at + tile, :] = (out / total).astype(jnp.bfloat16)
                block = jnp.where(lane == 2 * g, top, block)
                block = jnp.where(lane == 2 * g + 1, total, block)
            pieces.append(jnp.transpose(block)[:8])
        upper = lax.broadcasted_iota(jnp.int32, (8, width), 0) < 4
        firsts, seconds = [], []
        flat = jnp.concatenate(pieces, axis=1)
        for k in range(rows // width):
            x = flat[:, k * width : (k + 1) * width]
            high = x.astype(jnp.bfloat16).astype(jnp.float32)
            middle = (x - high).astype(jnp.bfloat16).astype(jnp.float32)
            firsts.append(jnp.where(upper, high, middle))
            seconds.append(x - high - middle)
        stats = jnp.concatenate(firsts + seconds, axis=0)
        out_ref[share * rows :, :] = stats.astype(jnp.bfloat16)


def remote_call(name, active, q, units, factor):
    share, rows, width = q.shape
    count = len(units)
    extra = 2 * 8 * (rows // width)
    any_space = pl.BlockSpec(memory_space=pl.ANY)
    flops = 4 * share * rows * rows * width * count
    return pl.pallas_call(
        functools.partial(remote_kernel, min(256, rows), factor, count),
        name=name,
        out_shape=jax.ShapeDtypeStruct((share * rows + extra, width), jnp.bfloat16),
        in_specs=[pl.BlockSpec(memory_space=pltpu.SMEM)] + [any_space] * (count + 1),
        out_specs=pl.BlockSpec(memory_space=pltpu.VMEM),
        scratch_shapes=[
            pltpu.VMEM((share, rows, width), jnp.bfloat16),
            pltpu.VMEM((count, 2, rows, width), jnp.bfloat16),
            pltpu.SemaphoreType.DMA((count + 1,)),
        ],
        cost_estimate=pl.CostEstimate(
            flops=flops, bytes_accessed=2 * q.size * (count + 2), transcendentals=0
        ),
    )(active, q, *units)


def local_kernel(tile, factor, groups, active, q_hbm, *refs):
    count = sum(groups) + 1
    units = refs[:count]
    out_ref, stat_ref, q_buf, kv_buf, sems = refs[count:]
    share, rows, width = q_buf.shape
    copies = [pltpu.make_async_copy(units[u], kv_buf.at[u], sems.at[u]) for u in range(count)]
    query_copy = pltpu.make_async_copy(q_hbm, q_buf, sems.at[count])
    query_copy.start()
    copies[0].start()
    members, first = [], 1
    for size in groups:
        members.append(list(range(first, first + size)))
        first += size
    for k, member in enumerate(members):

        @pl.when(active[k] > 0)
        def _():
            for u in member:
                copies[u].start()

    query_copy.wait()
    copies[0].wait()
    earlier = lax.broadcasted_iota(jnp.int32, (tile, tile), 0) >= lax.broadcasted_iota(
        jnp.int32, (tile, tile), 1
    )
    for g in range(share):
        for j in range(rows // tile):
            lo, hi = j * tile, (j + 1) * tile
            q = q_buf[g, lo:hi, :]
            parts = [jnp.where(earlier, dot_nt(q, kv_buf[0, 0, lo:hi, :]), NEG)]
            values = [kv_buf[0, 1, lo:hi, :]]
            if j:
                parts.append(dot_nt(q, kv_buf[0, 0, :lo, :]))
                values.append(kv_buf[0, 1, :lo, :])
            top = row_max(parts)
            total, out = soft(parts, values, top, factor)
            out_ref[g, lo:hi, :] = out
            stat_ref[0, g, lo:hi, :] = jnp.broadcast_to(top, (tile, 128))
            stat_ref[1, g, lo:hi, :] = jnp.broadcast_to(total, (tile, 128))
    for k, member in enumerate(members):

        @pl.when(active[k] > 0)
        def _():
            for u in member:
                copies[u].wait()
            for g in range(share):
                for j in range(rows // tile):
                    lo, hi = j * tile, (j + 1) * tile
                    q = q_buf[g, lo:hi, :]
                    parts = [dot_nt(q, kv_buf[u, 0]) for u in member]
                    before = stat_ref[0, g, lo:hi, 0:1]
                    top = jnp.maximum(before, row_max(parts))
                    total, out = soft(parts, [kv_buf[u, 1] for u in member], top, factor)
                    fade = jnp.exp2((before - top) * factor)
                    out_ref[g, lo:hi, :] = out_ref[g, lo:hi, :] * fade + out
                    total = stat_ref[1, g, lo:hi, 0:1] * fade + total
                    stat_ref[0, g, lo:hi, :] = jnp.broadcast_to(top, (tile, 128))
                    stat_ref[1, g, lo:hi, :] = jnp.broadcast_to(total, (tile, 128))


def local_call(name, active, q, own, groups, factor):
    share, rows, width = q.shape
    sizes = tuple(len(group) for group in groups)
    units = [own] + [unit for group in groups for unit in group]
    count = len(units)
    any_space = pl.BlockSpec(memory_space=pl.ANY)
    flops = 4 * share * rows * rows * width * count
    return pl.pallas_call(
        functools.partial(local_kernel, min(256, rows), factor, sizes),
        name=name,
        out_shape=(
            jax.ShapeDtypeStruct((share, rows, width), jnp.float32),
            jax.ShapeDtypeStruct((2, share, rows, 128), jnp.float32),
        ),
        in_specs=[pl.BlockSpec(memory_space=pltpu.SMEM)] + [any_space] * (count + 1),
        out_specs=(
            pl.BlockSpec(memory_space=pltpu.VMEM),
            pl.BlockSpec(memory_space=pltpu.VMEM),
        ),
        scratch_shapes=[
            pltpu.VMEM((share, rows, width), jnp.bfloat16),
            pltpu.VMEM((count, 2, rows, width), jnp.bfloat16),
            pltpu.SemaphoreType.DMA((count + 1,)),
        ],
        cost_estimate=pl.CostEstimate(
            flops=flops, bytes_accessed=2 * q.size * (count + 6), transcendentals=0
        ),
    )(active, q, *units)


def merge_kernel(heads, share, width, factor, info, *refs):
    out_ref = refs[-1]
    block = out_ref.shape[0]
    step = pl.program_id(0)
    per = width // block
    merged = []
    for h in range(heads):
        acc_ref, stat_ref = refs[2 * h], refs[2 * h + 1]
        base = 2 * heads + h * (share + 1)
        tail = refs[base + share][...].astype(jnp.float32)
        half = tail.shape[0] // 2
        firsts, seconds = tail[:half], tail[half:]
        first = jnp.zeros((8, block), jnp.float32)
        second = jnp.zeros((8, block), jnp.float32)
        for k in range(half // 8):
            for p in range(per):
                here = step == k * per + p
                cut = (slice(8 * k, 8 * k + 8), slice(p * block, (p + 1) * block))
                first = jnp.where(here, firsts[cut], first)
                second = jnp.where(here, seconds[cut], second)
        stats = first + pltpu.roll(first, 4, 0) + second
        columns = jnp.transpose(jnp.tile(stats, (128 // 8, 1)))
        use = info[h] > 0
        for g in range(share):
            top = stat_ref[0, g][:, 0:1]
            total = stat_ref[1, g][:, 0:1]
            acc = acc_ref[g]
            top_far = jnp.where(use, columns[:, 2 * g : 2 * g + 1], top)
            total_far = jnp.where(use, columns[:, 2 * g + 1 : 2 * g + 2], 0.0)
            far = jnp.where(use, refs[base + g][...].astype(jnp.float32), 0.0)
            newest = jnp.maximum(top, top_far)
            near_scale = jnp.exp2((top - newest) * factor)
            far_scale = jnp.exp2((top_far - newest) * factor) * total_far
            weight = 1.0 / (total * near_scale + far_scale)
            merged.append(acc * (near_scale * weight) + far * (far_scale * weight))
    stacked = jnp.stack(merged, axis=0)
    row = step * block + lax.broadcasted_iota(jnp.int32, (1, block, 1), 1)
    stacked = jnp.where(row < info[heads], stacked, 0.0).astype(jnp.bfloat16)
    out_ref[...] = jnp.transpose(stacked, (1, 0, 2))


def merge_call(info, locals_, fars, factor):
    share, rows, width = locals_[0][0].shape
    heads = len(locals_)
    block = 128
    in_specs = [pl.BlockSpec(memory_space=pltpu.SMEM)]
    operands = [info]
    for acc, stat in locals_:
        operands += [acc, stat]
        in_specs += [
            pl.BlockSpec((share, block, width), lambda i: (0, i, 0)),
            pl.BlockSpec((2, share, block, 128), lambda i: (0, 0, i, 0)),
        ]
    extra = fars[0].shape[0] - share * rows
    for far in fars:
        for g in range(share):
            operands.append(far)
            in_specs.append(
                pl.BlockSpec((block, width), lambda i, g=g: (g * (rows // block) + i, 0))
            )
        operands.append(far)
        in_specs.append(pl.BlockSpec((extra, width), lambda i: (share * rows // extra, 0)))
    return pl.pallas_call(
        functools.partial(merge_kernel, heads, share, width, factor),
        name="merge",
        grid=(rows // block,),
        out_shape=jax.ShapeDtypeStruct((rows, heads * share, width), jnp.bfloat16),
        in_specs=in_specs,
        out_specs=pl.BlockSpec((block, heads * share, width), lambda i: (i, 0, 0)),
    )(*operands)


def causal_shards(queries, key_heads, projected_value_heads, lengths):
    rows, head_count, width = queries.shape
    heads = key_heads.shape[1]
    share = head_count // heads
    factor = math.log2(math.e) * width ** (-0.5)
    me = lax.axis_index("seq")
    chip, core = me // 2, me % 2
    last = heads - 1

    def move(name, value, hops):
        pairs = [(2 * a + c, 2 * b + c) for a, b in hops for c in range(2)]
        with jax.named_scope(name):
            return lax.ppermute(value, "seq", pairs)

    def twin(name, value, chips):
        pairs = [(2 * a + c, 2 * a + 1 - c) for a in chips for c in range(2)]
        with jax.named_scope(name):
            return lax.ppermute(value, "seq", pairs)

    def flag(*conditions):
        return jnp.stack([jnp.asarray(c).astype(jnp.int32) for c in conditions])

    q = [queries[:, h * share : (h + 1) * share].transpose(1, 0, 2) for h in range(heads)]
    kv = [jnp.stack([key_heads[:, h], projected_value_heads[:, h]]) for h in range(heads)]

    across = [move(f"x{h}", kv[h], ((0, 1), (1, 0), (2, 3))) for h in range(last)]
    asked = [move(f"u{h}", q[h], ((2, 0), (3, 1))) for h in range(last)]
    down = move("d0", kv[last], ((0, 2), (1, 3)))
    side = move("s0", q[last], ((3, 2),))
    across.append(move(f"x{last}", kv[last], ((0, 1),)))
    own = [twin(f"t{h}", kv[h], (0, 1, 2, 3)) for h in range(heads)]
    across_twin = [twin(f"c{h}", across[h], (0, 1, 3)) for h in range(last)]
    across_twin.append(twin(f"c{last}", across[last], (1,)))
    down_twin = twin("e0", down, (2,))
    relay = move("r0", down, ((3, 2),))
    relay_twin = twin("e1", relay, (2,))

    front = flag(chip < 2)
    odd = (chip % 2) == 1
    locals_, fars = [], []
    for h in range(last):
        partial = remote_call(
            f"remote{h}", front, asked[h], [kv[h], own[h], across[h], across_twin[h]], factor
        )
        fars.append(move(f"o{h}", partial, ((0, 2), (1, 3))))
        locals_.append(
            local_call(
                f"local{h}",
                flag(core == 1, odd),
                q[h],
                kv[h],
                [[own[h]], [across[h], across_twin[h]]],
                factor,
            )
        )
    partial = remote_call(
        f"remote{last}",
        flag(chip == 2),
        side,
        [kv[last], own[last], down, down_twin, relay, relay_twin],
        factor,
    )
    fars.append(move(f"o{last}", partial, ((2, 3),)))
    locals_.append(
        local_call(
            f"local{last}",
            flag(core == 1, chip == 1, chip == 2),
            q[last],
            kv[last],
            [
                [own[last]],
                [across[last], across_twin[last]],
                [down, down_twin, relay, relay_twin],
            ],
            factor,
        )
    )
    info = flag(*([chip >= 2] * last + [chip == 3, lengths[0] - me * rows]))
    return merge_call(info, locals_, fars, factor)


def solution(mesh):
    ranks = mesh.shape["seq"]

    def shards(queries, key_heads, projected_value_heads, lengths):
        rows, head_count, width = queries.shape
        heads = key_heads.shape[1]
        split = (
            ranks == 8
            and ranks * rows <= WINDOW
            and head_count == 2 * heads
            and heads > 1
            and rows % 256 == 0
            and rows % width == 0
            and width % 128 == 0
        )
        plan = causal_shards if split else windowed_shards
        return plan(queries, key_heads, projected_value_heads, lengths)

    in_specs = (
        P(("batch", "seq"), None, None),
        P(("batch", "seq"), None, None),
        P(("batch", "seq"), None, None),
        P("batch"),
    )
    out_specs = P(("batch", "seq"), None, None)
    return jax.shard_map(shards, mesh=mesh, in_specs=in_specs, out_specs=out_specs, check_vma=False)
```
